32 devices in a mesh: skyx: 2 (over y), skyy: 4 (over x, core), freq: 4 (over z).
Axes of the slice: x: 2, y: 2, z: 4, core: 2. Of those that a mesh axis runs over, the one named last changes fastest.
Arguments:
- field: float32 [512, 8, 512], P('freq', 'skyx', 'skyy'), may hold values from -6 to 6
- noise: float32 [512, 8, 512], P('freq', 'skyx', 'skyy'), may hold values from -1.2 to 1.2
- step_size: float32 [512], P('freq'), may hold values from 0.35 to 0.6
- w_first: bfloat16 [3, 3, 64, 1], replicated, may hold values from -2 to 2
- w_second: bfloat16 [3, 3, 64, 64], replicated, may hold values from -0.25 to 0.25
- w_third: bfloat16 [3, 3, 64, 64], replicated, may hold values from -0.25 to 0.25
- w_last: bfloat16 [3, 3, 1, 64], replicated, may hold values from -0.25 to 0.25
- observed: float32 [512, 8, 512], P(None, ('skyx', 'freq'), 'skyy'), may hold values from -6 to 6
- inv_variance: float32 [512, 8, 512], P(None, ('skyx', 'freq'), 'skyy'), may hold values from 0.3 to 3
- offsets: int32 [8], P(('skyx', 'freq')), may hold values from 0 to 512
- beam_table: float32 [1024, 31], replicated, may hold values from -1 to 1
- kbin: int32 [8, 512], P(('skyx', 'freq'), 'skyy'), may hold values from 0 to 7
- wedge_taps: float32 [8, 31], replicated, may hold values from -1 to 1
Outputs:
- next_field: float32 [512, 8, 512], P('freq', 'skyx', 'skyy')
The draws below stay inside these ranges and needn't reach their ends.
Inputs may be any that keep to these rules, and one draw needn't show every extreme that they name: `offsets`: every offset plus 512 is at most 1024.
All inputs are finite; a program needn't handle non-finite values.
Results may differ from the reference program's by a relative error of at most 0.0045.
Values may be sent and summed in bfloat16 or wider, within the bound.
No kernel may reach another device: no remote copies, remote signals or barrier semaphores. Data moves between devices by JAX's collectives and lax.ppermute only.
A program may use at most 448 MiB of HBM per device.

```python
import math
import jax
import jax.numpy as jnp
from jax import lax

NF = 512
NCH = 1024
FEAT = 64
TAPS = 31
KBINS = 8
NX = 8
NY = 512


def touch_ends(result, key, least, top_value):
    longest = result.shape.index(max(result.shape))
    spots = []
    for shift in (0, 1):
        where = [jax.random.randint(jax.random.fold_in(key, axis), (), 0, length) for axis, length in enumerate(result.shape)]
        where[longest] = (where[longest] + shift) % result.shape[longest]
        spots.append(tuple(where))
    return result.at[spots[0]].set(least).at[spots[1]].set(top_value)


def block_scale(stream_key, shape, shards, least, top_value):
    gain, own = 1.0, jax.random.fold_in(stream_key, 6)
    for dim, blocks in shards:
        steps = jnp.exp(jax.random.uniform(jax.random.fold_in(own, dim), (blocks,), jnp.float32, least / len(shards), top_value / len(shards)))
        gain = gain * jnp.repeat(steps, shape[dim] // blocks).reshape([-1 if axis == dim else 1 for axis in range(len(shape))])
    return gain


def centred(rng, shape, width, reach, split=(), kind=jnp.bfloat16):
    loudness = block_scale(rng, shape, split, -0.22, 0.18) if split else 1.0
    values = jax.random.normal(rng, shape, jnp.float32) * width * loudness
    return jnp.minimum(jnp.maximum(values, -reach), reach).astype(kind)


def setup_inputs(seed: int = 0) -> dict:
    key_list = jax.random.split(jax.random.key(seed), 14)
    return {
        "field": centred(key_list[0], (NF, NX, NY), 1.0, 6.0, ((0, 4), (1, 2), (2, 4)), jnp.float32),
        "noise": centred(key_list[1], (NF, NX, NY), 0.2, 1.2, ((0, 4), (1, 2), (2, 4)), jnp.float32),
        "step_size": jnp.clip(jnp.exp(math.log(0.6) - 0.5389966 * jax.random.uniform(key_list[2], (NF,), jnp.float32) ** block_scale(key_list[2], (NF,), ((0, 4),), -0.2, 0.2)), 0.35, 0.6),
        "w_first": centred(key_list[3], (3, 3, FEAT, 1), 9 ** -0.5, 2.0),
        "w_second": centred(key_list[4], (3, 3, FEAT, FEAT), (2.0 * (9 * FEAT) ** -0.5), 0.25),
        "w_third": centred(key_list[5], (3, 3, FEAT, FEAT), (2.0 * (9 * FEAT) ** -0.5), 0.25),
        "w_last": centred(key_list[6], (3, 3, 1, FEAT), (2.0 * (9 * FEAT) ** -0.5), 0.25),
        "observed": centred(key_list[7], (NF, NX, NY), 1.0, 6.0, ((1, 8), (2, 4)), jnp.float32),
        "inv_variance": jnp.clip(jnp.exp(math.log(3.0) - 2.3025851 * jax.random.uniform(key_list[8], (NF, NX, NY), jnp.float32) ** block_scale(key_list[8], (NF, NX, NY), ((1, 8), (2, 4)), -0.2, 0.2)), 0.3, 3.0),
        "offsets": touch_ends(jax.random.randint(key_list[9], (NX,), 0, NCH - NF + 1), jax.random.fold_in(key_list[9], 1), 0, NCH - NF).astype(jnp.int32),
        "beam_table": centred(key_list[10], (NCH, TAPS), TAPS ** -0.5, 1.0, (), jnp.float32),
        "kbin": touch_ends(jax.random.randint(key_list[11], (NX, NY), 0, KBINS), jax.random.fold_in(key_list[11], 1), 0, KBINS - 1).astype(jnp.int32),
        "wedge_taps": centred(key_list[12], (KBINS, TAPS), TAPS ** -0.5, 1.0, (), jnp.float32),
    }


def conv_full(inputs, kernel):
    kern = jnp.transpose(kernel.astype(jnp.float32), (2, 3, 0, 1))
    return lax.conv_general_dilated(inputs, kern, (1, 1), ((1, 1), (1, 1)), precision=lax.Precision.HIGHEST)

def settle(values):
    rounded = lax.optimization_barrier(values.astype(jnp.bfloat16))
    return rounded.astype(jnp.float32)

def reference(field, noise, step_size, w_first, w_second, w_third, w_last, observed, inv_variance, offsets, beam_table, kbin, wedge_taps):
    xb = field.astype(jnp.bfloat16)

    def network(channel):
        inputs = channel.astype(jnp.float32)[None, None]
        hidden = settle(jax.nn.silu(conv_full(inputs, w_first)))
        hidden = settle(jax.nn.silu(conv_full(hidden, w_second)))
        hidden = settle(jax.nn.silu(conv_full(hidden, w_third)))
        return conv_full(hidden, w_last)[0, 0]
    score = lax.map(network, xb)
    half = TAPS // 2
    chans = NF
    index = offsets[:, None] + jnp.arange(chans, dtype=jnp.int32)[None, :]
    beam = beam_table[index]
    beam_t = jnp.transpose(beam, (2, 1, 0))
    spectra = xb.astype(jnp.float32)
    padded = jnp.pad(spectra, ((half, half), (0, 0), (0, 0)))
    model = jnp.zeros_like(spectra)
    for tap in range(TAPS):
        model = model + beam_t[tap][:, :, None] * padded[tap:tap + chans]
    resid = model - observed
    taps_px = jnp.transpose(wedge_taps[kbin], (2, 0, 1))
    padded = jnp.pad(resid, ((half, half), (0, 0), (0, 0)))
    wedged = jnp.zeros_like(resid)
    for tap in range(TAPS):
        wedged = wedged + taps_px[tap][None] * padded[tap:tap + chans]
    weighted = inv_variance * wedged
    padded = jnp.pad(weighted, ((half, half), (0, 0), (0, 0)))
    back = jnp.zeros_like(weighted)
    for tap in range(TAPS):
        back = back + taps_px[tap][None] * padded[2 * half - tap:2 * half - tap + chans]
    back_pad = jnp.pad(back, ((half, half), (0, 0), (0, 0)))
    beam_pad = jnp.pad(beam_t, ((0, 0), (half, half), (0, 0)))
    grad = jnp.zeros_like(back)
    for tap in range(TAPS):
        product = beam_pad[tap][:, :, None] * back_pad
        grad = grad + product[2 * half - tap:2 * half - tap + chans]
    grad = grad.astype(jnp.bfloat16).astype(jnp.float32)
    steps = step_size[:, None, None]
    return field + steps * (score - grad) + jnp.sqrt(2.0 * steps) * noise
```

```python
import functools

import jax
import jax.numpy as jnp
import numpy as np
from jax import lax
from jax.experimental import pallas as pl
from jax.experimental.pallas import tpu as pltpu
from jax.sharding import PartitionSpec as P

TAPS = 31
KBINS = 8
BF = jnp.bfloat16
F32 = jnp.float32
LANES = 128
GROUP = 16
PITCH = 32


def padded_2(block, sides, width):
    for axis, dim in sides:
        count = lax.axis_size(axis)
        forward = [(i, i + 1) for i in range(count - 1)]
        backward = [(target, source) for source, target in forward]
        low = lax.ppermute(
            lax.slice_in_dim(block, block.shape[dim] - width, None, axis=dim), axis, forward
        )
        high = lax.ppermute(lax.slice_in_dim(block, 0, width, axis=dim), axis, backward)
        block = jnp.concatenate([low, block, high], axis=dim)
    return block


def conv_local(padded, kernel):
    height = padded.shape[2] - 2
    width = padded.shape[3] - 2
    total = None
    for row_tap in range(3):
        for col_tap in range(3):
            window = padded[:, :, row_tap : row_tap + height, col_tap : col_tap + width]
            term = jnp.einsum(
                "oc,fchw->fohw",
                kernel[row_tap, col_tap],
                window,
                preferred_element_type=jnp.float32,
            )
            total = term if total is None else total + term
    return total


def with_rim(values):
    return padded_2(values, (("skyx", 2), ("skyy", 3)), 1)


def plain_score(xb, w_first, w_second, w_third, w_last):
    hidden = xb[:, None]
    for kernel in (w_first, w_second, w_third):
        hidden = jax.nn.silu(conv_local(with_rim(hidden), kernel)).astype(jnp.bfloat16)
    return conv_local(with_rim(hidden), w_last)[:, 0]


def silu_half(u):
    return (u + u * jnp.tanh(u)).astype(BF)


def net_body(tiles_x, tiles_y, rows_loc, chans, cols_loc, chunk,
             x_ref, base_ref, w2_ref, w3_ref, wl_ref, out_ref,
             x1_ref, w1_ref, w2s_ref, w3s_ref, h1_ref, h2_ref, nb_ref, h3_ref, ot_ref):
    rows = tiles_x * rows_loc
    cols = tiles_y * cols_loc
    pairs = cols // 2
    groups = cols // GROUP
    per_block = cols_loc // GROUP
    feat = w2_ref.shape[-1]
    two = 2 * feat
    lane = lax.broadcasted_iota(jnp.int32, (chans, LANES), 1)

    k_row = lax.broadcasted_iota(jnp.int32, (4 * PITCH, 16), 0)
    k_col = lax.broadcasted_iota(jnp.int32, (4 * PITCH, 16), 1)
    base = base_ref[...]
    for p in range(GROUP // 2):
        pick = (k_row // PITCH == k_col // 4) & (k_row % PITCH == k_col % 4 + 2 * p)
        w1_ref[p] = jnp.dot(pick.astype(BF), base, preferred_element_type=F32).astype(BF)

    zero = jnp.zeros((feat, feat), BF)
    for src, dst in ((w2_ref, w2s_ref), (w3_ref, w3s_ref)):
        for w in range(4):
            for blk in range(4):
                for a in range(2):
                    ta = w - a
                    parts = []
                    for b in range(2):
                        tb = (1 - b, 2 - b, 3 - b, -b)[blk]
                        ok = 0 <= ta < 3 and 0 <= tb < 3
                        parts.append(src[ta * 3 + tb] if ok else zero)
                    k0 = (w * 4 + blk) * feat
                    dst[k0 : k0 + feat, a * two : (a + 1) * two] = jnp.concatenate(parts, axis=1)

    rim = jnp.zeros((rows, 1, chans, two), BF)
    for ref in (h1_ref, h2_ref):
        ref[:, 0:1] = rim
        ref[:, pairs + 1 : pairs + 2] = rim
    edge = jnp.zeros((ot_ref.shape[0], LANES), F32)
    ot_ref[:, 0:LANES] = edge
    ot_ref[:, LANES + pairs * chans :] = edge

    def window_block(cb, _):
        lo = jnp.maximum(cb - 1, 0)
        hi = jnp.minimum(cb + 1, tiles_y - 1)
        has_lo = (cb > 0).astype(F32)
        has_hi = (cb < tiles_y - 1).astype(F32)
        for gl in range(per_block):
            acc = [jnp.zeros((chans, LANES), F32) for _ in range(rows // 2)]
            for r in range(rows):
                src = (r // rows_loc) * tiles_y
                rl = r % rows_loc
                cur = x_ref[(src + cb) * rows_loc + rl].astype(F32)
                for w in range(4):
                    rb = r + 1 - w
                    if rb % 2 or not 0 <= rb < rows:
                        continue
                    shift = (PITCH * w - (GROUP * gl - 1)) % LANES
                    val = pltpu.roll(cur, shift, 1)
                    if gl == 0:
                        prev = x_ref[(src + lo) * rows_loc + rl].astype(F32) * has_lo
                        val = jnp.where(lane == PITCH * w, pltpu.roll(prev, shift, 1), val)
                    if gl == per_block - 1:
                        nxt = x_ref[(src + hi) * rows_loc + rl].astype(F32) * has_hi
                        val = jnp.where(
                            lane == PITCH * w + GROUP + 1, pltpu.roll(nxt, shift, 1), val
                        )
                    keep = (lane >= PITCH * w) & (lane < PITCH * w + GROUP + 2)
                    acc[rb // 2] = jnp.where(keep, val, acc[rb // 2])
            for half in range(rows // 2):
                x1_ref[half, cb * per_block + gl] = acc[half].astype(BF)
        return 0

    lax.fori_loop(0, tiles_y, window_block, 0)

    def first(step, _):
        half = step // (GROUP // 2)
        p = step % (GROUP // 2)
        lhs = x1_ref[half].reshape(groups * chans, 4 * PITCH)
        u = jnp.dot(lhs, w1_ref[p], preferred_element_type=F32)
        h = silu_half(u).reshape(groups, chans, 2 * two)
        for g in range(groups):
            for a in range(2):
                h1_ref[2 * half + a, 1 + g * (GROUP // 2) + p] = h[g, :, a * two : (a + 1) * two]
        return 0

    lax.fori_loop(0, (rows // 2) * (GROUP // 2), first, 0)

    lane_nb = lax.broadcasted_iota(jnp.int32, (chunk, chans, two), 2)

    def layer(src, weights, start, emit):
        for r in range(rows):
            nb_ref[r] = jnp.where(
                lane_nb < feat, src[r, pl.ds(start + 2, chunk)], src[r, pl.ds(start, chunk)]
            )
        for rb in range(0, rows, 2):
            first_w = 1 if rb == 0 else 0
            last_w = 3 if rb + 2 >= rows else 4
            parts = []
            for w in range(first_w, last_w):
                r = rb - 1 + w
                parts.append(src[r, pl.ds(start + 1, chunk)].reshape(chunk * chans, two))
                parts.append(nb_ref[r].reshape(chunk * chans, two))
            lhs = jnp.concatenate(parts, axis=1)
            u = jnp.dot(
                lhs, weights[first_w * 2 * two : last_w * 2 * two], preferred_element_type=F32
            )
            h = silu_half(u)
            for a in range(2):
                emit(rb + a, h[:, a * two : (a + 1) * two].reshape(chunk, chans, two))

    def second(step, _):
        start = step * chunk

        def emit(r, h):
            h2_ref[r, pl.ds(start + 1, chunk)] = h

        layer(h1_ref, w2s_ref, start, emit)
        return 0

    lax.fori_loop(0, pairs // chunk, second, 0)

    def third(step, _):
        start = step * chunk

        def emit(r, h):
            h3_ref[r] = h

        layer(h2_ref, w3s_ref, start, emit)
        full = jnp.concatenate(
            [h3_ref[r].reshape(chunk * chans, two) for r in range(rows)], axis=1
        )
        out = lax.dot_general(
            wl_ref[...], full, (((1,), (1,)), ((), ())), preferred_element_type=F32
        )
        width = chunk * chans
        ot_ref[:, pl.ds(pl.multiple_of(LANES + step * width, LANES), width)] = out
        return 0

    lax.fori_loop(0, pairs // chunk, third, 0)

    own_rows = 2 * rows
    per_tile = 2 * rows_loc
    width = (cols_loc // 2) * chans
    sub = lax.broadcasted_iota(jnp.int32, (own_rows, width), 0) % per_tile
    for ty in range(tiles_y):
        at = LANES + ty * width
        own = ot_ref[:own_rows, at : at + width]
        before = ot_ref[own_rows:, at - chans : at - chans + width]
        after = ot_ref[own_rows:, at + chans : at + chans + width]
        total = own + jnp.where(sub < rows_loc, before, after)
        for tx in range(tiles_x):
            out_ref[tx * tiles_y + ty] = total[tx * per_tile : (tx + 1) * per_tile].astype(BF)


def net_constants(w_first, w_second, w_third, w_last, rows, rows_loc):
    feat = w_second.shape[-1]
    half = jnp.asarray(0.5, BF)
    first = (w_first[..., 0] * half).astype(BF)
    base = jnp.stack(
        [
            jnp.pad(first, ((a, 1 - a), (b, 1 - b), (0, 0)))
            for a in range(2)
            for b in range(2)
        ],
        axis=2,
    ).reshape(16, 4 * feat)
    second = jnp.swapaxes(w_second * half, 2, 3).reshape(9, feat, feat)
    third = jnp.swapaxes(w_third * half, 2, 3).reshape(9, feat, feat)
    pick = np.zeros((2, rows // rows_loc, 2, rows_loc, rows, 2, 9), np.float32)
    for r_out in range(rows):
        for r_in in range(max(r_out - 1, 0), min(r_out + 2, rows)):
            ta = r_in - r_out + 1
            for b_in in range(2):
                for b in range(2):
                    tile, rl = divmod(r_out, rows_loc)
                    pick[0, tile, b, rl, r_in, b_in, ta * 3 + b_in - b + 1] = 1
                    tb = b_in - 1 if b == 0 else b_in + 2
                    if 0 <= tb < 3:
                        pick[1, tile, b, rl, r_in, b_in, ta * 3 + tb] = 1
    last = jnp.dot(
        jnp.asarray(pick.reshape(-1, 9), BF),
        w_last.reshape(9, feat),
        preferred_element_type=F32,
    ).astype(BF).reshape(4 * rows, rows * 2 * feat)
    return base, second, third, last


def net_score(spread, consts, tiles_x, tiles_y, rows_loc, interpret=False):
    base, second, third, last = consts
    chans, cols_loc = spread.shape[1:]
    feat = second.shape[-1]
    rows = tiles_x * rows_loc
    cols = tiles_y * cols_loc
    pairs = cols // 2
    chunk = next(c for c in (32, 16, 8) if pairs % c == 0)
    groups = cols // GROUP
    vmem = pltpu.MemorySpace.VMEM
    spec = pl.BlockSpec(memory_space=vmem)
    return pl.pallas_call(
        functools.partial(net_body, tiles_x, tiles_y, rows_loc, chans, cols_loc, chunk),
        out_shape=jax.ShapeDtypeStruct(
            (tiles_x * tiles_y, 2 * rows_loc, cols_loc // 2 * chans), BF
        ),
        in_specs=[spec] * 5,
        out_specs=spec,
        scratch_shapes=[
            pltpu.VMEM((rows // 2, groups, chans, 4 * PITCH), BF),
            pltpu.VMEM((GROUP // 2, 4 * PITCH, 4 * feat), BF),
            pltpu.VMEM((16 * feat, 4 * feat), BF),
            pltpu.VMEM((16 * feat, 4 * feat), BF),
            pltpu.VMEM((rows, pairs + 2, chans, 2 * feat), BF),
            pltpu.VMEM((rows, pairs + 2, chans, 2 * feat), BF),
            pltpu.VMEM((rows, chunk, chans, 2 * feat), BF),
            pltpu.VMEM((rows, chunk, chans, 2 * feat), BF),
            pltpu.VMEM((4 * rows, 2 * LANES + pairs * chans), F32),
        ],
        compiler_params=pltpu.CompilerParams(vmem_limit_bytes=58 << 20),
        name="net",
        interpret=interpret,
    )(spread, base, second, third, last)


PAD = 16


def spec_body(chans, block, x_ref, beam_ref, obs_ref, var_ref, kbin_ref, taps_ref, out_ref,
              xp_ref, rp_ref, wp_ref, bp_ref, bb_ref, tap_ref):
    half = TAPS // 2
    cols = x_ref.shape[-1]
    edge = jnp.zeros((PAD, cols), F32)
    for ref in (xp_ref, rp_ref, wp_ref, bp_ref):
        ref[0:PAD] = edge
        ref[PAD + chans :] = edge
    for tap in range(TAPS):
        bb_ref[tap, 0:PAD] = edge
        bb_ref[tap, PAD + chans :] = edge
    xp_ref[PAD : PAD + chans] = x_ref[...].astype(F32)
    bins = kbin_ref[...]
    for tap in range(TAPS):
        val = jnp.zeros((1, cols), F32)
        for k in range(KBINS):
            val = jnp.where(bins == k, taps_ref[k, tap], val)
        tap_ref[tap : tap + 1] = val
    steps = chans // block

    def span(start):
        return pl.ds(start, block)

    def model(i, _):
        f0 = pl.multiple_of(i * block, block)
        acc = jnp.zeros((block, cols), F32)
        beam = beam_ref[span(f0)]
        for tap in range(TAPS):
            wide = jnp.broadcast_to(beam[:, tap : tap + 1], (block, cols))
            bb_ref[tap, span(PAD + f0)] = wide
            acc = acc + wide * xp_ref[span(f0 + PAD - half + tap)]
        rp_ref[span(PAD + f0)] = acc - obs_ref[span(f0)]
        return 0

    lax.fori_loop(0, steps, model, 0)

    def wedge(i, _):
        f0 = pl.multiple_of(i * block, block)
        acc = jnp.zeros((block, cols), F32)
        for tap in range(TAPS):
            acc = acc + tap_ref[tap : tap + 1] * rp_ref[span(f0 + PAD - half + tap)]
        wp_ref[span(PAD + f0)] = acc * var_ref[span(f0)]
        return 0

    lax.fori_loop(0, steps, wedge, 0)

    def back(i, _):
        f0 = pl.multiple_of(i * block, block)
        acc = jnp.zeros((block, cols), F32)
        for tap in range(TAPS):
            acc = acc + tap_ref[tap : tap + 1] * wp_ref[span(f0 + PAD + half - tap)]
        bp_ref[span(PAD + f0)] = acc
        return 0

    lax.fori_loop(0, steps, back, 0)

    def grad(i, _):
        f0 = pl.multiple_of(i * block, block)
        acc = jnp.zeros((block, cols), F32)
        for tap in range(TAPS):
            at = span(f0 + PAD + half - tap)
            acc = acc + bb_ref[tap, at] * bp_ref[at]
        out_ref[span(f0)] = acc.astype(BF)
        return 0

    lax.fori_loop(0, steps, grad, 0)


def spec_grad(spectra, beam, observed, inv_variance, kbin, wedge_taps, interpret=False):
    chans, cols = spectra.shape
    spec = pl.BlockSpec(memory_space=pltpu.MemorySpace.VMEM)
    smem = pl.BlockSpec(memory_space=pltpu.MemorySpace.SMEM)
    tall = pltpu.VMEM((chans + 2 * PAD, cols), F32)
    return pl.pallas_call(
        functools.partial(spec_body, chans, 64 if chans % 64 == 0 else 8),
        out_shape=jax.ShapeDtypeStruct((chans, cols), BF),
        in_specs=[spec] * 5 + [smem],
        out_specs=spec,
        scratch_shapes=[
            tall, tall, tall, tall,
            pltpu.VMEM((TAPS, chans + 2 * PAD, cols), F32),
            pltpu.VMEM((TAPS + 1, cols), F32),
        ],
        compiler_params=pltpu.CompilerParams(vmem_limit_bytes=32 << 20),
        name="spectral",
        interpret=interpret,
    )(spectra, beam, observed, inv_variance, kbin, wedge_taps)


def start_body(rows_loc, field_ref, out_ref):
    chans = out_ref.shape[1]
    for r in range(rows_loc):
        out_ref[r] = field_ref[pl.ds(r, chans, stride=rows_loc)].astype(BF)


def row_major(field, interpret=False):
    chans, rows_loc, cols = field.shape
    spec = pl.BlockSpec(memory_space=pltpu.MemorySpace.VMEM)
    return pl.pallas_call(
        functools.partial(start_body, rows_loc),
        out_shape=jax.ShapeDtypeStruct((rows_loc, chans, cols), BF),
        in_specs=[spec],
        out_specs=spec,
        name="rows",
        interpret=interpret,
    )(field.reshape(chans * rows_loc, cols))


def last_body(rows_loc, field_ref, noise_ref, step_ref, grad_ref, score_ref, out_ref, lhs_ref):
    sources, _, wide = score_ref.shape
    chans, cols = grad_ref.shape[1:]
    sub = chans // sources
    mine = lax.broadcasted_iota(jnp.int32, (sub, wide), 1) % sub == lax.broadcasted_iota(
        jnp.int32, (sub, wide), 0
    )
    k = lax.broadcasted_iota(jnp.int32, (2 * wide, cols), 0)
    c = lax.broadcasted_iota(jnp.int32, (2 * wide, cols), 1)
    place = (2 * ((k % wide) // sub) + k // wide == c).astype(F32).astype(BF)
    zero = jnp.zeros((sub, wide), F32)
    for s in range(sources):
        block = score_ref[s].astype(F32)
        for r in range(rows_loc):
            for b in range(2):
                row = block[b * rows_loc + r : b * rows_loc + r + 1]
                lhs_ref[r, s * sub : (s + 1) * sub, b * wide : (b + 1) * wide] = jnp.where(
                    mine, jnp.broadcast_to(row, (sub, wide)), zero
                ).astype(BF)
    step = jnp.broadcast_to(step_ref[...], (chans, cols))
    spread = jnp.sqrt(2.0 * step)
    for r in range(rows_loc):
        score = jnp.dot(lhs_ref[r], place, preferred_element_type=F32)
        at = pl.ds(r, chans, stride=rows_loc)
        out_ref[at] = (
            field_ref[at]
            + step * (score - grad_ref[r].astype(F32))
            + spread * noise_ref[at]
        )


def finish(field, noise, step_size, grad, score, interpret=False):
    chans, rows_loc, cols = field.shape
    spec = pl.BlockSpec(memory_space=pltpu.MemorySpace.VMEM)
    wide = score.shape[-1]
    out = pl.pallas_call(
        functools.partial(last_body, rows_loc),
        out_shape=jax.ShapeDtypeStruct((chans * rows_loc, cols), F32),
        in_specs=[spec] * 5,
        out_specs=spec,
        scratch_shapes=[pltpu.VMEM((rows_loc, chans, 2 * wide), BF)],
        name="finish",
        interpret=interpret,
    )(
        field.reshape(chans * rows_loc, cols),
        noise.reshape(chans * rows_loc, cols),
        step_size[:, None],
        grad,
        score,
    )
    return out.reshape(chans, rows_loc, cols)


def per_device(
    field,
    noise,
    step_size,
    w_first,
    w_second,
    w_third,
    w_last,
    observed,
    inv_variance,
    offsets,
    beam_table,
    kbin,
    wedge_taps,
):
    chans_loc, rows_loc, cols_loc = field.shape
    tiles_x, tiles_y = lax.axis_size("skyx"), lax.axis_size("skyy")
    tiles = tiles_x * tiles_y
    freq = lax.axis_size("freq")
    chans = observed.shape[0]
    rows_spec = observed.shape[1]
    fast = (
        chans_loc % (16 * tiles) == 0
        and rows_loc % 2 == 0
        and cols_loc % LANES == 0
        and 2 * w_second.shape[-1] == LANES
        and chans_loc // tiles * tiles_x * rows_loc * tiles_y * cols_loc <= 1 << 16
    )

    rows_first = row_major(field)
    if fast:
        spread = lax.all_to_all(
            rows_first.reshape(rows_loc, chans_loc, cols_loc),
            ("skyx", "skyy"), split_axis=1, concat_axis=0, tiled=True,
        )
    spectra = lax.all_to_all(rows_first, "freq", split_axis=0, concat_axis=0, tiled=True)
    spectra = spectra.reshape(freq, rows_spec, chans_loc, cols_loc)

    grads = []
    for r in range(rows_spec):
        beam = lax.dynamic_slice(beam_table, (offsets[r], 0), (chans, TAPS))
        grads.append(
            spec_grad(
                spectra[:, r].reshape(chans, cols_loc),
                beam,
                observed[:, r],
                inv_variance[:, r],
                kbin[r : r + 1],
                wedge_taps,
            ).reshape(freq, chans_loc, cols_loc)
        )
    grad = jnp.stack(grads, axis=1).reshape(freq * rows_spec, chans_loc, cols_loc)
    grad = lax.all_to_all(grad, "freq", split_axis=0, concat_axis=0, tiled=True)

    if fast:
        consts = net_constants(
            w_first, w_second, w_third, w_last, tiles_x * rows_loc, rows_loc
        )
        score = net_score(spread, consts, tiles_x, tiles_y, rows_loc)
        score = lax.all_to_all(score, ("skyx", "skyy"), split_axis=0, concat_axis=0, tiled=True)
        return finish(field, noise, step_size, grad, score)
    score = plain_score(field.astype(BF), w_first, w_second, w_third, w_last)
    steps = step_size[:, None, None]
    grad = jnp.swapaxes(grad, 0, 1).astype(F32)
    return field + steps * (score - grad) + jnp.sqrt(2.0 * steps) * noise


def solution(mesh):
    return jax.shard_map(
        per_device,
        mesh=mesh,
        in_specs=(
            P("freq", "skyx", "skyy"),
            P("freq", "skyx", "skyy"),
            P("freq"),
            P(),
            P(),
            P(),
            P(),
            P(None, ("skyx", "freq"), "skyy"),
            P(None, ("skyx", "freq"), "skyy"),
            P(("skyx", "freq")),
            P(),
            P(("skyx", "freq"), "skyy"),
            P(),
        ),
        out_specs=P("freq", "skyx", "skyy"),
        check_vma=False,
    )
```

```python
import functools

import jax
import jax.numpy as jnp
import numpy as np
from jax import lax
from jax.experimental import pallas as pl
from jax.experimental.pallas import tpu as pltpu
from jax.sharding import PartitionSpec as P

TAPS = 31
KBINS = 8
BF = jnp.bfloat16
F32 = jnp.float32
LANES = 128
GROUP = 16
PITCH = 32


def padded_2(block, sides, width):
    for axis, dim in sides:
        count = lax.axis_size(axis)
        forward = [(i, i + 1) for i in range(count - 1)]
        backward = [(target, source) for source, target in forward]
        low = lax.ppermute(
            lax.slice_in_dim(block, block.shape[dim] - width, None, axis=dim), axis, forward
        )
        high = lax.ppermute(lax.slice_in_dim(block, 0, width, axis=dim), axis, backward)
        block = jnp.concatenate([low, block, high], axis=dim)
    return block


def conv_local(padded, kernel):
    height = padded.shape[2] - 2
    width = padded.shape[3] - 2
    total = None
    for row_tap in range(3):
        for col_tap in range(3):
            window = padded[:, :, row_tap : row_tap + height, col_tap : col_tap + width]
            term = jnp.einsum(
                "oc,fchw->fohw",
                kernel[row_tap, col_tap],
                window,
                preferred_element_type=jnp.float32,
            )
            total = term if total is None else total + term
    return total


def with_rim(values):
    return padded_2(values, (("skyx", 2), ("skyy", 3)), 1)


def plain_score(xb, w_first, w_second, w_third, w_last):
    hidden = xb[:, None]
    for kernel in (w_first, w_second, w_third):
        hidden = jax.nn.silu(conv_local(with_rim(hidden), kernel)).astype(jnp.bfloat16)
    return conv_local(with_rim(hidden), w_last)[:, 0]


def silu_half(u):
    return (u + u * jnp.tanh(u)).astype(BF)


def mate(index, step, count):
    if count & (count - 1) == 0:
        return index ^ step
    return (step - index) % count


def step_to(index, peer, count):
    if count & (count - 1) == 0:
        return index ^ peer
    return (index + peer) % count


def exchange(pieces, axis):
    count = len(pieces)
    got = []
    for d, piece in enumerate(pieces):
        pairs = [(i, mate(i, d, count)) for i in range(count)]
        if all(s == t for s, t in pairs):
            got.append(piece)
        else:
            got.append(lax.ppermute(piece, axis, pairs))
    return got


def vmem():
    return pl.BlockSpec(memory_space=pltpu.MemorySpace.VMEM)


def smem():
    return pl.BlockSpec(memory_space=pltpu.MemorySpace.SMEM)


def choose(scalar, options):
    out = options[0]
    for i, option in enumerate(options[1:], 1):
        out = jnp.where(scalar == i, option, out)
    return out


PAD = 16


class Chain:
    def __init__(self, chans, cols, beam, obs, var, scratch):
        self.chans, self.cols = chans, cols
        self.beam, self.obs, self.var = beam, obs, var
        self.xp, self.rp, self.wp, self.bp, self.bb, self.tap, self.out = scratch

    @staticmethod
    def scratch(chans, cols):
        tall = pltpu.VMEM((chans + 2 * PAD, cols), F32)
        return [
            tall, tall, tall, tall,
            pltpu.VMEM((TAPS, chans + 2 * PAD, cols), F32),
            pltpu.VMEM((TAPS + 1, cols), F32),
            pltpu.VMEM((chans, cols), BF),
        ]

    def begin(self, pieces, me, kbin_ref, taps_ref):
        edge = jnp.zeros((PAD, self.cols), F32)
        for ref in (self.xp, self.rp, self.wp, self.bp):
            ref[0:PAD] = edge
            ref[PAD + self.chans :] = edge
        for tap in range(TAPS):
            self.bb[tap, 0:PAD] = edge
            self.bb[tap, PAD + self.chans :] = edge
        count = len(pieces)
        part = self.chans // count
        for d, piece in enumerate(pieces):
            at = pl.multiple_of(PAD + mate(me, d, count) * part, 8)
            self.xp[pl.ds(at, part)] = piece[...].astype(F32)
        bins = kbin_ref[...]
        for tap in range(TAPS):
            val = jnp.zeros((1, self.cols), F32)
            for k in range(KBINS):
                val = jnp.where(bins == k, taps_ref[k, tap], val)
            self.tap[tap : tap + 1] = val

    def model(self, f0, block):
        acc = jnp.zeros((block, self.cols), F32)
        beam = self.beam[pl.ds(f0, block)]
        for tap in range(TAPS):
            wide = jnp.broadcast_to(beam[:, tap : tap + 1], (block, self.cols))
            self.bb[tap, pl.ds(PAD + f0, block)] = wide
            acc = acc + wide * self.xp[pl.ds(f0 + PAD - TAPS // 2 + tap, block)]
        self.rp[pl.ds(PAD + f0, block)] = acc - self.obs[pl.ds(f0, block)]

    def wedge(self, f0, block):
        acc = jnp.zeros((block, self.cols), F32)
        for tap in range(TAPS):
            acc = acc + self.tap[tap : tap + 1] * self.rp[pl.ds(f0 + PAD - TAPS // 2 + tap, block)]
        self.wp[pl.ds(PAD + f0, block)] = acc * self.var[pl.ds(f0, block)]

    def back(self, f0, block):
        acc = jnp.zeros((block, self.cols), F32)
        for tap in range(TAPS):
            acc = acc + self.tap[tap : tap + 1] * self.wp[pl.ds(f0 + PAD + TAPS // 2 - tap, block)]
        self.bp[pl.ds(PAD + f0, block)] = acc

    def grad(self, f0, block):
        acc = jnp.zeros((block, self.cols), F32)
        for tap in range(TAPS):
            at = pl.ds(f0 + PAD + TAPS // 2 - tap, block)
            acc = acc + self.bb[tap, at] * self.bp[at]
        self.out[pl.ds(f0, block)] = acc.astype(BF)

    def finish(self, outs, me):
        count = len(outs)
        part = self.chans // count
        for d, out in enumerate(outs):
            at = pl.multiple_of(mate(me, d, count) * part, 16)
            out[...] = self.out[pl.ds(at, part)]


def spec_body(count, chans, block, *refs):
    pieces, refs = refs[:count], refs[count:]
    me_ref, beam, obs, var, kbin, taps = refs[:6]
    outs, scratch = refs[6 : 6 + count], refs[6 + count :]
    chain = Chain(chans, obs.shape[-1], beam, obs, var, scratch)
    me = me_ref[0]
    chain.begin(pieces, me, kbin, taps)
    for stage in (chain.model, chain.wedge, chain.back, chain.grad):

        def step(i, _, stage=stage):
            stage(pl.multiple_of(i * block, block), block)
            return 0

        lax.fori_loop(0, chans // block, step, 0)
    chain.finish(outs, me)


def spec_grad(pieces, me, beam, observed, inv_variance, kbin, wedge_taps, interpret=False):
    chans, cols = observed.shape
    count = len(pieces)
    return pl.pallas_call(
        functools.partial(spec_body, count, chans, 64 if chans % 64 == 0 else 16),
        out_shape=[jax.ShapeDtypeStruct((chans // count, cols), BF)] * count,
        in_specs=[vmem()] * count + [smem()] + [vmem()] * 4 + [smem()],
        out_specs=[vmem()] * count,
        scratch_shapes=Chain.scratch(chans, cols),
        compiler_params=pltpu.CompilerParams(vmem_limit_bytes=16 << 20),
        name="spectral",
        interpret=interpret,
    )(*pieces, me, beam, observed, inv_variance, kbin, wedge_taps)


def prep_body(tiles_x, tiles_y, rows_loc, chans, cols_loc,
              x_ref, wa_ref, wb_ref, wc_ref, wd_ref, pick_ref,
              x1_ref, w1_ref, w2s_ref, w3s_ref, wl_ref, nine_ref):
    rows = tiles_x * rows_loc
    per_block = cols_loc // GROUP
    feat = wb_ref.shape[-1]
    two = 2 * feat
    lane = lax.broadcasted_iota(jnp.int32, (chans, LANES), 1)

    def nine(ref, scale):
        nine_ref[...] = jnp.zeros(nine_ref.shape, F32)
        for ta in range(3):
            nine_ref[3 * ta : 3 * ta + 3] = ref[ta].astype(F32) * scale
        return nine_ref[...].astype(BF)

    got = jnp.dot(pick_ref[...], nine(wd_ref, 1.0), preferred_element_type=F32)
    n_out = 4 * rows
    for r in range(rows):
        at = 2 * r * n_out
        wl_ref[:, r * two : (r + 1) * two] = jnp.concatenate(
            [got[at : at + n_out], got[at + n_out : at + 2 * n_out]], axis=1
        ).astype(BF)

    first = nine(wa_ref, 0.5)
    blank = jnp.zeros((16, feat), BF)
    base = jnp.concatenate(
        [
            jnp.concatenate([first if i == j else blank for j in range(4)], axis=1)
            for i in range(4)
        ],
        axis=0,
    )
    k_row = lax.broadcasted_iota(jnp.int32, (4 * PITCH, 64), 0)
    k_col = lax.broadcasted_iota(jnp.int32, (4 * PITCH, 64), 1)
    tap = k_col % 16
    row_ok = (tap < 9) & (k_row // PITCH - k_col // 32 == tap // 3)
    col_gap = k_row % PITCH - (k_col // 16) % 2 - tap % 3
    for p in range(GROUP // 2):
        pick = jnp.where(row_ok & (col_gap == 2 * p), 1.0, 0.0).astype(BF)
        w1_ref[p] = jnp.dot(pick, base, preferred_element_type=F32).astype(BF)

    zero = jnp.zeros((feat, feat), F32)
    for src, dst in ((wb_ref, w2s_ref), (wc_ref, w3s_ref)):
        flip = [
            [jnp.transpose(src[ta, tb].astype(F32) * 0.5) for tb in range(3)] for ta in range(3)
        ]
        for w in range(4):
            for blk in range(4):
                for a in range(2):
                    ta = w - a
                    parts = []
                    for b in range(2):
                        tb = (1 - b, 2 - b, 3 - b, -b)[blk]
                        parts.append(flip[ta][tb] if 0 <= ta < 3 and 0 <= tb < 3 else zero)
                    k0 = (w * 4 + blk) * feat
                    dst[k0 : k0 + feat, a * two : (a + 1) * two] = jnp.concatenate(
                        parts, axis=1
                    ).astype(BF)

    def window_block(cb, _):
        lo = jnp.maximum(cb - 1, 0)
        hi = jnp.minimum(cb + 1, tiles_y - 1)
        has_lo = (cb > 0).astype(F32)
        has_hi = (cb < tiles_y - 1).astype(F32)
        for gl in range(per_block):
            acc = [jnp.zeros((chans, LANES), F32) for _ in range(rows // 2)]
            for r in range(rows):
                src = (r // rows_loc) * tiles_y
                rl = r % rows_loc
                cur = x_ref[src + cb, rl].astype(F32)
                for w in range(4):
                    rb = r + 1 - w
                    if rb % 2 or not 0 <= rb < rows:
                        continue
                    shift = (PITCH * w - (GROUP * gl - 1)) % LANES
                    val = pltpu.roll(cur, shift, 1)
                    if gl == 0:
                        prev = x_ref[src + lo, rl].astype(F32) * has_lo
                        val = jnp.where(lane == PITCH * w, pltpu.roll(prev, shift, 1), val)
                    if gl == per_block - 1:
                        nxt = x_ref[src + hi, rl].astype(F32) * has_hi
                        val = jnp.where(
                            lane == PITCH * w + GROUP + 1, pltpu.roll(nxt, shift, 1), val
                        )
                    keep = (lane >= PITCH * w) & (lane < PITCH * w + GROUP + 2)
                    acc[rb // 2] = jnp.where(keep, val, acc[rb // 2])
            for half in range(rows // 2):
                x1_ref[half, cb * per_block + gl] = acc[half].astype(BF)
        return 0

    lax.fori_loop(0, tiles_y, window_block, 0)


def last_pick(rows, rows_loc):
    pick = np.zeros((rows, 2, 2, rows // rows_loc, 2, rows_loc, 16), np.float32)
    for r_out in range(rows):
        tile, rl = divmod(r_out, rows_loc)
        for r_in in range(max(r_out - 1, 0), min(r_out + 2, rows)):
            ta = r_in - r_out + 1
            for b_in in range(2):
                for b in range(2):
                    pick[r_in, b_in, 0, tile, b, rl, ta * 3 + b_in - b + 1] = 1
                    tb = b_in - 1 if b == 0 else b_in + 2
                    if 0 <= tb < 3:
                        pick[r_in, b_in, 1, tile, b, rl, ta * 3 + tb] = 1
    return jnp.asarray(pick.reshape(-1, 16), BF)


def prep(spread, w_first, w_second, w_third, w_last, tiles_x, tiles_y, interpret=False):
    _, rows_loc, chans, cols_loc = spread.shape
    feat = w_second.shape[-1]
    rows = tiles_x * rows_loc
    groups = tiles_y * cols_loc // GROUP
    return pl.pallas_call(
        functools.partial(prep_body, tiles_x, tiles_y, rows_loc, chans, cols_loc),
        out_shape=[
            jax.ShapeDtypeStruct((rows // 2, groups, chans, 4 * PITCH), BF),
            jax.ShapeDtypeStruct((GROUP // 2, 4 * PITCH, 4 * feat), BF),
            jax.ShapeDtypeStruct((16 * feat, 4 * feat), BF),
            jax.ShapeDtypeStruct((16 * feat, 4 * feat), BF),
            jax.ShapeDtypeStruct((4 * rows, rows * 2 * feat), BF),
        ],
        in_specs=[vmem()] * 6,
        out_specs=[vmem()] * 5,
        scratch_shapes=[pltpu.VMEM((16, feat), F32)],
        compiler_params=pltpu.CompilerParams(vmem_limit_bytes=8 << 20),
        name="prep",
        interpret=interpret,
    )(spread, w_first[..., 0], w_second, w_third, w_last[:, :, 0], last_pick(rows, rows_loc))


def net_body(tiles_x, tiles_y, rows_loc, cols_loc, chunk, count, *refs):
    x1_ref, w1_ref, w2s_ref, w3s_ref, wl_ref = refs[:5]
    pieces, refs = refs[5 : 5 + count], refs[5 + count :]
    me_ref, beam, obs, var, kbin, taps, out_ref = refs[:7]
    grads, refs = refs[7 : 7 + count], refs[7 + count :]
    h1_ref, h2_ref, nb_ref, h3_ref, ot_ref = refs[:5]
    chain = Chain(*obs.shape, beam, obs, var, refs[5:])
    rows = tiles_x * rows_loc
    pairs = tiles_y * cols_loc // 2
    groups, chans = x1_ref.shape[1:3]
    two = h1_ref.shape[-1]
    feat = two // 2
    me = me_ref[0]
    chain.begin(pieces, me, kbin, taps)

    rim = jnp.zeros((rows, 1, chans, two), BF)
    for ref in (h1_ref, h2_ref):
        ref[:, 0:1] = rim
        ref[:, pairs + 1 : pairs + 2] = rim
    edge = jnp.zeros((ot_ref.shape[0], LANES), F32)
    ot_ref[:, 0:LANES] = edge
    ot_ref[:, LANES + pairs * chans :] = edge

    def first(half, _):
        lhs = x1_ref[half].reshape(groups * chans, 4 * PITCH)
        for p in range(GROUP // 2):
            u = jnp.dot(lhs, w1_ref[p], preferred_element_type=F32)
            h = silu_half(u).reshape(groups, chans, 2 * two)
            for g in range(groups):
                for a in range(2):
                    h1_ref[2 * half + a, 1 + g * (GROUP // 2) + p] = h[
                        g, :, a * two : (a + 1) * two
                    ]
        return 0

    lax.fori_loop(0, rows // 2, first, 0)

    lane_nb = lax.broadcasted_iota(jnp.int32, (chunk, chans, two), 2)

    def layer(src, weights, start, emit):
        for r in range(rows):
            nb_ref[r] = jnp.where(
                lane_nb < feat, src[r, pl.ds(start + 2, chunk)], src[r, pl.ds(start, chunk)]
            )
        for rb in range(0, rows, 2):
            first_w = 1 if rb == 0 else 0
            last_w = 3 if rb + 2 >= rows else 4
            parts = []
            for w in range(first_w, last_w):
                r = rb - 1 + w
                parts.append(src[r, pl.ds(start + 1, chunk)].reshape(chunk * chans, two))
                parts.append(nb_ref[r].reshape(chunk * chans, two))
            lhs = jnp.concatenate(parts, axis=1)
            u = jnp.dot(
                lhs, weights[first_w * 2 * two : last_w * 2 * two], preferred_element_type=F32
            )
            h = silu_half(u)
            for a in range(2):
                emit(rb + a, h[:, a * two : (a + 1) * two].reshape(chunk, chans, two))

    def second(step):
        start = step * chunk

        def emit(r, h):
            h2_ref[r, pl.ds(start + 1, chunk)] = h

        layer(h1_ref, w2s_ref, start, emit)

    def third(step):
        start = step * chunk

        def emit(r, h):
            h3_ref[r] = h

        layer(h2_ref, w3s_ref, start, emit)
        full = jnp.concatenate(
            [h3_ref[r].reshape(chunk * chans, two) for r in range(rows)], axis=1
        )
        out = lax.dot_general(
            wl_ref[...], full, (((1,), (1,)), ((), ())), preferred_element_type=F32
        )
        width = chunk * chans
        ot_ref[:, pl.ds(pl.multiple_of(LANES + step * width, LANES), width)] = out

    steps = pairs // chunk
    portion = chain.chans // (steps // 2)
    block = next(b for b in (64, 32, 16, 8) if portion % b == 0)
    for run, stages in ((second, (chain.model, chain.wedge)), (third, (chain.back, chain.grad))):
        for half, stage in enumerate(stages):

            def step(i, _, run=run, half=half, stage=stage):
                run(i + half * (steps // 2))
                for k in range(portion // block):
                    stage(pl.multiple_of(i * portion, portion) + k * block, block)
                return 0

            lax.fori_loop(0, steps // 2, step, 0)
    chain.finish(grads, me)

    own_rows = 2 * rows
    per_tile = 2 * rows_loc
    width = (cols_loc // 2) * chans
    sub = lax.broadcasted_iota(jnp.int32, (own_rows, width), 0) % per_tile
    for ty in range(tiles_y):
        at = LANES + ty * width
        own = ot_ref[:own_rows, at : at + width]
        before = ot_ref[own_rows:, at - chans : at - chans + width]
        after = ot_ref[own_rows:, at + chans : at + chans + width]
        total = own + jnp.where(sub < rows_loc, before, after)
        for tx in range(tiles_x):
            out_ref[tx * tiles_y + ty] = total[tx * per_tile : (tx + 1) * per_tile].astype(BF)


def net_chunk(pairs):
    return next((c for c in (32, 16, 8) if pairs % (2 * c) == 0), 0)


def net(ready, pieces, me, beam, observed, inv_variance, kbin, wedge_taps,
        tiles_x, tiles_y, rows_loc, cols_loc, interpret=False):
    chans = ready[0].shape[2]
    two = ready[2].shape[1] // 2
    rows = tiles_x * rows_loc
    pairs = tiles_y * cols_loc // 2
    chunk = net_chunk(pairs)
    count = len(pieces)
    long, cols = observed.shape
    out = pl.pallas_call(
        functools.partial(net_body, tiles_x, tiles_y, rows_loc, cols_loc, chunk, count),
        out_shape=[
            jax.ShapeDtypeStruct((tiles_x * tiles_y, 2 * rows_loc, cols_loc // 2 * chans), BF)
        ]
        + [jax.ShapeDtypeStruct((long // count, cols), BF)] * count,
        in_specs=[vmem()] * (5 + count) + [smem()] + [vmem()] * 4 + [smem()],
        out_specs=[vmem()] * (1 + count),
        scratch_shapes=[
            pltpu.VMEM((rows, pairs + 2, chans, two), BF),
            pltpu.VMEM((rows, pairs + 2, chans, two), BF),
            pltpu.VMEM((rows, chunk, chans, two), BF),
            pltpu.VMEM((rows, chunk, chans, two), BF),
            pltpu.VMEM((4 * rows, 2 * LANES + pairs * chans), F32),
        ]
        + Chain.scratch(long, cols),
        compiler_params=pltpu.CompilerParams(vmem_limit_bytes=44 << 20),
        name="net",
        interpret=interpret,
    )(*ready, *pieces, me, beam, observed, inv_variance, kbin, wedge_taps)
    return out[0], out[1:]


def rows_body(rows_loc, count, field_ref, me_ref, sky_ref, *outs):
    chans, cols = outs[0].shape[1:]
    tiles, _, sub, _ = sky_ref.shape
    me = me_ref[0]
    rows = []
    for r in range(rows_loc):
        row = field_ref[pl.ds(r, chans, stride=rows_loc)].astype(BF)
        sky_ref[:, r] = row.reshape(tiles, sub, cols)
        rows.append(row)
    per = rows_loc // count
    for d, out in enumerate(outs):
        for r in range(per):
            out[r] = choose(mate(me, d, count), [rows[q * per + r] for q in range(count)])


def row_split(field, me, tiles, count, interpret=False):
    chans, rows_loc, cols = field.shape
    out = pl.pallas_call(
        functools.partial(rows_body, rows_loc, count),
        out_shape=[jax.ShapeDtypeStruct((tiles, rows_loc, chans // tiles, cols), BF)]
        + [jax.ShapeDtypeStruct((rows_loc // count, chans, cols), BF)] * count,
        in_specs=[vmem(), smem()],
        out_specs=[vmem()] * (1 + count),
        compiler_params=pltpu.CompilerParams(vmem_limit_bytes=4 << 20),
        name="rows",
        interpret=interpret,
    )(field.reshape(chans * rows_loc, cols), me)
    return out[0], out[1:]


def join_body(rows_loc, field_ref, noise_ref, step_ref, score_ref, out_ref, wide_ref, lhs_ref):
    sources, _, wide = score_ref.shape
    chans, cols = out_ref.shape[1:]
    sub = chans // sources
    mine = lax.broadcasted_iota(jnp.int32, (sub, wide), 1) % sub == lax.broadcasted_iota(
        jnp.int32, (sub, wide), 0
    )
    k = lax.broadcasted_iota(jnp.int32, (2 * wide, cols), 0)
    c = lax.broadcasted_iota(jnp.int32, (2 * wide, cols), 1)
    place = jnp.where(2 * ((k % wide) // sub) + k // wide == c, 1.0, 0.0).astype(BF)
    zero = jnp.zeros((sub, wide), F32)
    for s in range(sources):
        block = score_ref[s].astype(F32)
        for r in range(rows_loc):
            for b in range(2):
                row = block[b * rows_loc + r : b * rows_loc + r + 1]
                lhs_ref[r, s * sub : (s + 1) * sub, b * wide : (b + 1) * wide] = jnp.where(
                    mine, jnp.broadcast_to(row, (sub, wide)), zero
                ).astype(BF)
    step = jnp.transpose(jnp.broadcast_to(step_ref[...], (cols, chans)))
    wide_ref[...] = step
    spread = jnp.sqrt(2.0 * step)
    for r in range(rows_loc):
        score = jnp.dot(lhs_ref[r], place, preferred_element_type=F32)
        at = pl.ds(r, chans, stride=rows_loc)
        out_ref[r] = field_ref[at] + step * score + spread * noise_ref[at]


def join(field, noise, step_size, score, interpret=False):
    chans, rows_loc, cols = field.shape
    wide = score.shape[-1]
    return pl.pallas_call(
        functools.partial(join_body, rows_loc),
        out_shape=[
            jax.ShapeDtypeStruct((rows_loc, chans, cols), F32),
            jax.ShapeDtypeStruct((chans, cols), F32),
        ],
        in_specs=[vmem()] * 4,
        out_specs=[vmem()] * 2,
        scratch_shapes=[pltpu.VMEM((rows_loc, chans, 2 * wide), BF)],
        compiler_params=pltpu.CompilerParams(vmem_limit_bytes=8 << 20),
        name="join",
        interpret=interpret,
    )(
        field.reshape(chans * rows_loc, cols),
        noise.reshape(chans * rows_loc, cols),
        step_size[None],
        score,
    )


def last_body(count, part_ref, wide_ref, me_ref, *refs):
    grads, out_ref = refs[:count], refs[count]
    rows_loc, chans = part_ref.shape[:2]
    per = rows_loc // count
    me = me_ref[0]
    step = wide_ref[...]
    for r in range(rows_loc):
        grad = choose(step_to(me, r // per, count), [g[r % per] for g in grads])
        out_ref[pl.ds(r, chans, stride=rows_loc)] = part_ref[r] - step * grad.astype(F32)


def last(part, wide, me, grads, interpret=False):
    rows_loc, chans, cols = part.shape
    count = len(grads)
    out = pl.pallas_call(
        functools.partial(last_body, count),
        out_shape=jax.ShapeDtypeStruct((chans * rows_loc, cols), F32),
        in_specs=[vmem()] * 2 + [smem()] + [vmem()] * count,
        out_specs=vmem(),
        compiler_params=pltpu.CompilerParams(vmem_limit_bytes=4 << 20),
        name="last",
        interpret=interpret,
    )(part, wide, me, *grads)
    return out.reshape(chans, rows_loc, cols)


def per_device(
    field,
    noise,
    step_size,
    w_first,
    w_second,
    w_third,
    w_last,
    observed,
    inv_variance,
    offsets,
    beam_table,
    kbin,
    wedge_taps,
):
    chans_loc, rows_loc, cols_loc = field.shape
    tiles_x, tiles_y = lax.axis_size("skyx"), lax.axis_size("skyy")
    tiles = tiles_x * tiles_y
    freq = lax.axis_size("freq")
    chans, rows_spec = observed.shape[:2]
    me = lax.axis_index("freq").astype(jnp.int32)[None]
    chunk = net_chunk(tiles_y * cols_loc // 2)
    steps = tiles_y * cols_loc // 2 // chunk if chunk else 0
    fast = (
        chans_loc % (16 * tiles) == 0
        and rows_loc % 2 == 0
        and rows_spec == 1
        and cols_loc == LANES
        and 2 * w_second.shape[-1] == LANES
        and steps > 0
        and chans % (8 * steps // 2) == 0
        and chans_loc // tiles * tiles_x * rows_loc * tiles_y * cols_loc <= 1 << 16
    )

    sky, pieces = row_split(field, me, tiles if fast else 1, freq)
    if fast:
        spread = lax.all_to_all(
            sky, ("skyx", "skyy"), split_axis=0, concat_axis=0, tiled=True
        )
    pieces = exchange(pieces, "freq")
    beams = [
        lax.dynamic_slice(beam_table, (offsets[r], 0), (chans, TAPS)) for r in range(rows_spec)
    ]
    rest = [
        (beams[r], observed[:, r], inv_variance[:, r], kbin[r : r + 1], wedge_taps)
        for r in range(rows_spec)
    ]
    if fast:
        ready = prep(spread, w_first, w_second, w_third, w_last, tiles_x, tiles_y)
        score, grads = net(
            ready, [p[0] for p in pieces], me, *rest[0], tiles_x, tiles_y, rows_loc, cols_loc
        )
        score = lax.all_to_all(score, ("skyx", "skyy"), split_axis=0, concat_axis=0, tiled=True)
        grads = exchange([g[None] for g in grads], "freq")
        part, wide = join(field, noise, step_size, score)
        return last(part, wide, me, grads)
    each = [spec_grad([p[r] for p in pieces], me, *rest[r]) for r in range(rows_spec)]
    grads = exchange([jnp.stack(parts) for parts in zip(*each)], "freq")
    score = plain_score(field.astype(BF), w_first, w_second, w_third, w_last)
    steps = step_size[:, None, None]
    part = field + steps * score + jnp.sqrt(2.0 * steps) * noise
    wide = jnp.broadcast_to(step_size[:, None], (chans_loc, cols_loc))
    return last(jnp.swapaxes(part, 0, 1), wide, me, grads)


def solution(mesh):
    return jax.shard_map(
        per_device,
        mesh=mesh,
        in_specs=(
            P("freq", "skyx", "skyy"),
            P("freq", "skyx", "skyy"),
            P("freq"),
            P(),
            P(),
            P(),
            P(),
            P(None, ("skyx", "freq"), "skyy"),
            P(None, ("skyx", "freq"), "skyy"),
            P(("skyx", "freq")),
            P(),
            P(("skyx", "freq"), "skyy"),
            P(),
        ),
        out_specs=P("freq", "skyx", "skyy"),
        check_vma=False,
    )
```
